768 devices in a mesh: seq: 192 (over y, z, core), section: 4 (over x).
Axes of the slice: x: 4, y: 8, z: 12, core: 2. Of those that a mesh axis runs over, the one named last changes fastest.
Arguments:
- stream_in: bfloat16 [4, 24576, 2048], P('section', 'seq'), may hold values from -20 to 20
- keys_values: bfloat16 [4, 2, 24576, 512], P('section', None, 'seq'), may hold values from -6 to 6
- out_weight: bfloat16 [4, 2048, 2048], P('section'), may hold values from -1 to 1
- tile_mask: int32 [4, 16, 16], P('section'), may hold values 0 or 1
- cotangent: bfloat16 [4, 24576, 2048], P('section', 'seq'), may hold values from -6 to 6
Outputs:
- stream_out: bfloat16 [4, 24576, 2048], P('section', 'seq')
- stream_grads: bfloat16 [4, 24576, 2048], P('section', 'seq')
- kv_grads: float32 [4, 2, 24576, 512], P('section', None, 'seq')
The draws below stay inside these ranges and needn't reach their ends.
All inputs are finite; a program needn't handle non-finite values. No bound on the sum of `tile_mask` on one device may be relied on, other than what follows from the above.
Results may differ from the reference program's by a relative error of at most 0.013.
Values may be sent and summed in bfloat16 or wider, within the bound.
A program may use at most 64 MiB of HBM per device.

```python
import jax
import jax.numpy as jnp
from jax import lax

HEADS = 16
KVH = 4
HD = 128
TILE = 128
TOK_DEV = 128
HID = 2048
KVW = 512
NT = 16
TOKENS = 24576
WINDOW = 256
LAYERS = 4


def draw_stream_in(key, part):
    shape = (LAYERS, TOKENS, HID)
    base = jnp.clip(jax.random.normal(key, shape, jnp.float32), -6.0, 6.0)
    return base.astype(jnp.bfloat16)


def draw_keys_values(key, part):
    shape = (LAYERS, 2, TOKENS, KVW)
    base = jnp.clip(jax.random.normal(key, shape, jnp.float32), -6.0, 6.0)
    return base.astype(jnp.bfloat16)


def with_ends(values, own_key, low, largest):
    dims = values.shape
    spot = [jax.random.randint(jax.random.fold_in(own_key, axis), (), 0, dims[axis]) for axis in range(len(dims))]
    values = values.at[tuple(spot)].set(low)
    longest = dims.index(max(dims))
    spot[longest] = (spot[longest] + 1) % dims[longest]
    return values.at[tuple(spot)].set(largest)


def level_of(stream_key, shape, pieces, smallest, top_value):
    def one(position, blocks):
        draws = jax.random.uniform(jax.random.fold_in(jax.random.fold_in(stream_key, 6), position), (blocks,), jnp.float32, smallest / len(pieces), top_value / len(pieces))
        return jnp.repeat(jnp.exp(draws), shape[position] // blocks).reshape((-1,) + (1,) * (len(shape) - position - 1))

    factor_of = one(*pieces[0])
    for cut in pieces[1:]:
        factor_of = factor_of * one(*cut)
    return factor_of


def noise(key, extent, scale, most, pieces=(), kind=jnp.bfloat16):
    entries = scale * jax.random.normal(key, extent, jnp.float32)
    if pieces:
        entries = entries * level_of(key, extent, pieces, -0.22, 0.18)
    return jnp.clip(entries, -most, most).astype(kind)


def setup_inputs(seed: int = 0) -> dict:
    seeds = jax.random.split(jax.random.key(seed), 6)
    return {
        "stream_in": draw_stream_in(jax.random.fold_in(seeds[5], 71), 0),
        "keys_values": draw_keys_values(jax.random.fold_in(seeds[5], 71), 0),
        "out_weight": noise(seeds[2], (LAYERS, HID, HID), (HID // 64) ** -0.5, 1.0, ((0, 4),)),
        "tile_mask": with_ends((jax.random.randint(seeds[3], (LAYERS, NT, NT), 0, 2) < 1).astype(jnp.int32), jax.random.fold_in(seeds[3], 1), 0, 1),
        "cotangent": noise(seeds[4], (LAYERS, TOKENS, HID), 1.0, 6.0, ((0, 4), (1, 192))),
    }


def pruned_weight(weight, tiles):
    tile_count = tiles.shape[0]
    shaped = weight.reshape(tile_count, TILE, tile_count, TILE)
    kept = jnp.where(tiles[:, None, :, None] > 0, shaped, jnp.zeros_like(shaped))
    return kept.reshape(weight.shape)


def band_softmax(q_heads, key_rows, row_pos, key_pos):
    logits = jnp.einsum('rkgd,jkd->kgrj', q_heads.astype(jnp.float32), key_rows.astype(jnp.float32)) * (HD ** -0.5)
    distance = row_pos[:, None] - key_pos[None, :]
    inside = (distance >= 0) & (distance < WINDOW) & (key_pos[None, :] >= 0)
    logits = jnp.where(inside[None, None], logits, -jnp.inf)
    row_top = jnp.max(logits, axis=-1, keepdims=True)
    exp_terms = jnp.exp(logits - row_top)
    return exp_terms / jnp.sum(exp_terms, axis=-1, keepdims=True)


def reference(stream_in, keys_values, out_weight, tile_mask, cotangent):
    block_rows = 4 * TOK_DEV
    block_total = TOKENS // block_rows
    block_ids = jnp.arange(block_total, dtype=jnp.int32)
    layer_outs = []
    in_grads = []
    kv_grads = []
    for layer in range(LAYERS):
        weight = pruned_weight(out_weight[layer], tile_mask[layer])
        padded = jnp.concatenate([jnp.zeros((2, WINDOW, KVW), jnp.bfloat16), keys_values[layer]], axis=1)
        stream = stream_in[layer]
        grad_in = cotangent[layer]
        d_attended = jnp.dot(grad_in, weight.T, preferred_element_type=jnp.float32).astype(jnp.bfloat16)

        def block_step(accum, block_id):
            row_start = (block_id * block_rows).astype(jnp.int32)
            queries = lax.dynamic_slice_in_dim(stream, row_start, block_rows, 0)
            kv_block = lax.dynamic_slice_in_dim(padded, row_start, block_rows + WINDOW, 1)
            row_pos = row_start + jnp.arange(block_rows, dtype=jnp.int32)
            key_pos = row_start - WINDOW + jnp.arange(block_rows + WINDOW, dtype=jnp.int32)
            q_heads = queries.reshape(block_rows, KVH, HEADS // KVH, HD)
            key_rows = kv_block[0].reshape(block_rows + WINDOW, KVH, HD)
            value_rows = kv_block[1].reshape(block_rows + WINDOW, KVH, HD)
            probs = band_softmax(q_heads, key_rows, row_pos, key_pos)
            prob_b = lax.optimization_barrier(probs.astype(jnp.bfloat16)).astype(jnp.float32)
            attended = jnp.einsum('kgrj,jkd->rkgd', prob_b, value_rows.astype(jnp.float32))
            attended = attended.astype(jnp.bfloat16).reshape(block_rows, HID)
            d_block = lax.dynamic_slice_in_dim(d_attended, row_start, block_rows, 0)
            d_heads = lax.optimization_barrier(d_block).astype(jnp.float32).reshape(block_rows, KVH, HEADS // KVH, HD)
            d_probs = jnp.einsum('rkgd,jkd->kgrj', d_heads, value_rows.astype(jnp.float32))
            d_values = jnp.einsum('kgrj,rkgd->jkd', prob_b, d_heads)
            row_dot = jnp.sum(probs * d_probs, axis=-1, keepdims=True)
            d_logits = (probs * (d_probs - row_dot)).astype(jnp.bfloat16)
            d_logits = lax.optimization_barrier(d_logits).astype(jnp.float32)
            d_queries = jnp.einsum('kgrj,jkd->rkgd', d_logits, key_rows.astype(jnp.float32)) * (HD ** -0.5)
            d_keys = jnp.einsum('kgrj,rkgd->jkd', d_logits, q_heads.astype(jnp.float32)) * (HD ** -0.5)
            update = jnp.stack([d_keys, d_values]).reshape(2, block_rows + WINDOW, KVW)
            current = lax.dynamic_slice_in_dim(accum, row_start, block_rows + WINDOW, 1)
            accum = lax.dynamic_update_slice_in_dim(accum, current + update, row_start, 1)
            return accum, (attended, d_queries.reshape(block_rows, HID))

        accum_zero = jnp.zeros((2, WINDOW + TOKENS, KVW), jnp.float32)
        accum, results = lax.scan(block_step, accum_zero, block_ids)
        attended = results[0].reshape(TOKENS, HID)
        d_queries = results[1].reshape(TOKENS, HID)
        mixed_rows = jnp.dot(attended, weight, preferred_element_type=jnp.float32)
        layer_outs.append((stream.astype(jnp.float32) + mixed_rows).astype(jnp.bfloat16))
        in_grads.append((grad_in.astype(jnp.float32) + d_queries).astype(jnp.bfloat16))
        kv_grads.append(accum[:, WINDOW:])
    stream_out = jnp.roll(jnp.stack(layer_outs), 1, axis=0)
    stream_grads = jnp.roll(jnp.stack(in_grads), -1, axis=0)
    return stream_out, stream_grads, jnp.stack(kv_grads)
```

```python
import functools

import jax
import jax.numpy as jnp
from jax import lax
from jax.experimental import pallas as pl
from jax.experimental.pallas import tpu as pltpu
from jax.sharding import PartitionSpec as P

HD = 128
MESH = pl.DeviceIdType.MESH
NT = (((1,), (1,)), ((), ()))
NN = (((1,), (0,)), ((), ()))


def dot(a, b, dims=NN):
    return lax.dot_general(a, b, dims, preferred_element_type=jnp.float32)


def cols(start, count=1):
    return pl.ds(start * HD, count * HD)


def kernel(
    n_seq, n_sec,
    x_hbm, kv_hbm, w_hbm, mask, cot_hbm,
    so, sg, kvg,
    x, cot, w, kv, kvin, datt, att, gsend, osend, kvsend, kvrecv, kvacc,
    lsem, wsem, kv_s, kv_r, gkv_s, gkv_r, g_s, g_r, o_s, o_r,
):
    seq, sec = lax.axis_index("seq"), lax.axis_index("section")
    groups = kv.shape[2] // HD
    heads = x.shape[1] // HD // groups
    tiles = x.shape[1] // HD
    width = heads * HD
    scale = HD ** -0.5
    to_exp2 = scale * 1.4426950408889634
    ahead = [lax.rem(seq + 1, n_seq), lax.rem(seq + 2, n_seq)]
    behind = [lax.rem(seq + n_seq - 1, n_seq), lax.rem(seq + n_seq - 2, n_seq)]
    up, down = lax.rem(sec + 1, n_sec), lax.rem(sec + n_sec - 1, n_sec)

    loads = [
        pltpu.make_async_copy(kv_hbm.at[0], kv, lsem.at[0]),
        pltpu.make_async_copy(cot_hbm.at[0], cot, lsem.at[1]),
        pltpu.make_async_copy(x_hbm.at[0], x, lsem.at[2]),
    ]
    wloads = [
        pltpu.make_async_copy(w_hbm.at[0, cols(g * heads, heads)], w.at[cols(g * heads, heads)], wsem.at[g])
        for g in range(groups)
    ]
    for copy in loads + wloads:
        copy.start()

    barrier = pltpu.get_barrier_semaphore()
    for peer in ahead + behind:
        pl.semaphore_signal(barrier, inc=1, device_id={"seq": peer}, device_id_type=MESH)
    for peer in (up, down):
        pl.semaphore_signal(barrier, inc=1, device_id={"section": peer}, device_id_type=MESH)
    pl.semaphore_wait(barrier, 6)

    kv_out = [[None] * groups for _ in range(2)]
    for g in range(groups):
        for d in range(2):
            kv_out[d][g] = pltpu.make_async_remote_copy(
                src_ref=kv_hbm.at[0, :, :, cols(g)],
                dst_ref=kvin.at[d, :, :, cols(g)],
                send_sem=kv_s.at[d, g],
                recv_sem=kv_r.at[d, g],
                device_id={"seq": ahead[d]},
                device_id_type=MESH,
            )
            kv_out[d][g].start()

    loads[1].wait()
    cot_v = cot[...]
    for g in range(groups):
        wloads[g].wait()
        for a in range(g * heads, (g + 1) * heads):
            for b in range(tiles):
                keep = mask[0, a, b].astype(jnp.float32).astype(jnp.bfloat16)
                w[cols(a), cols(b)] = w[cols(a), cols(b)] * keep
        full = dot(w[cols(g * heads, heads), :], cot_v, NT).astype(jnp.bfloat16)
        for h in range(heads):
            datt[:, cols(g * heads + h)] = full[h * HD : (h + 1) * HD]

    loads[0].wait()
    loads[2].wait()
    key = lax.broadcasted_iota(jnp.int32, (HD, width), 0)
    tok = lax.broadcasted_iota(jnp.int32, (HD, width), 1) % HD
    own = key <= tok
    low = jnp.float32(-1e30)
    bias1 = jnp.where(seq >= 1, jnp.float32(0), low)
    bias2 = jnp.where(seq >= 2, jnp.float32(0), low)
    zero = jnp.zeros((HD, width), jnp.bfloat16)

    def split(block, prev):
        return jnp.concatenate(
            [jnp.where(own, block, zero), prev, jnp.where(own, zero, block)], axis=0
        )

    g_out, gkv_out = [], []

    def forward(g):
        for d in range(2):
            kv_out[d][g].wait_recv()
        ks = jnp.concatenate([kv[0, :, cols(g)], kvin[0, 0, :, cols(g)], kvin[1, 0, :, cols(g)]], axis=0)
        vs = jnp.concatenate([kv[1, :, cols(g)], kvin[0, 1, :, cols(g)], kvin[1, 1, :, cols(g)]], axis=0)
        qs = jnp.concatenate([x[:, cols(g * heads + h)] for h in range(heads)], axis=0)
        s = dot(ks, qs, NT)
        sc = jnp.where(own, s[:HD], s[2 * HD :] + bias2)
        s1 = s[HD : 2 * HD] + bias1
        top = jnp.maximum(jnp.max(sc, axis=0, keepdims=True), jnp.max(s1, axis=0, keepdims=True))
        ec = jnp.exp2((sc - top) * to_exp2)
        e1 = jnp.exp2((s1 - top) * to_exp2)
        inv = 1.0 / (jnp.sum(ec, axis=0, keepdims=True) + jnp.sum(e1, axis=0, keepdims=True))
        pc, p1 = ec * inv, e1 * inv
        pb = split(pc.astype(jnp.bfloat16), p1.astype(jnp.bfloat16))
        out_t = dot(vs.T, pb).astype(jnp.bfloat16)
        for h in range(heads):
            att[:, cols(g * heads + h)] = out_t[:, h * HD : (h + 1) * HD].T
        return ks, vs, qs, pc, p1, pb

    def backward(g, ks, vs, qs, pc, p1, pb):
        dt = datt[:, cols(g * heads, heads)]
        dp = dot(vs, dt)
        dc, d1 = jnp.where(own, dp[:HD], dp[2 * HD :]), dp[HD : 2 * HD]
        row = jnp.sum(pc * dc, axis=0, keepdims=True) + jnp.sum(p1 * d1, axis=0, keepdims=True)
        ds = split((pc * (dc - row)).astype(jnp.bfloat16), (p1 * (d1 - row)).astype(jnp.bfloat16))
        dq_t = dot(ks.T, ds) * scale
        for h in range(heads):
            at = cols(g * heads + h)
            gsend[:, at] = (cot[:, at].astype(jnp.float32) + dq_t[:, h * HD : (h + 1) * HD].T).astype(jnp.bfloat16)
        copy = pltpu.make_async_remote_copy(
            src_ref=gsend.at[:, cols(g * heads, heads)],
            dst_ref=sg.at[0, :, cols(g * heads, heads)],
            send_sem=g_s.at[g],
            recv_sem=g_r.at[g],
            device_id={"section": down},
            device_id_type=MESH,
        )
        copy.start()
        g_out.append(copy)
        both = [dot(ds, qs) * scale, dot(pb, dt, NT)]
        for i in range(2):
            kvacc[i, :, cols(g)] = both[i][:HD]
            for d in range(2):
                kvsend[d, i, :, cols(g)] = both[i][(d + 1) * HD : (d + 2) * HD].astype(jnp.bfloat16)
        for d in range(2):
            copy = pltpu.make_async_remote_copy(
                src_ref=kvsend.at[d, :, :, cols(g)],
                dst_ref=kvrecv.at[d, :, :, cols(g)],
                send_sem=gkv_s.at[d, g],
                recv_sem=gkv_r.at[d, g],
                device_id={"seq": behind[d]},
                device_id_type=MESH,
            )
            copy.start()
            gkv_out.append(copy)

    for g in range(groups - 1):
        backward(g, *forward(g))
    held = forward(groups - 1)
    o_out = []
    for c in range(groups):
        at = cols(c * heads, heads)
        osend[:, at] = (x[:, at].astype(jnp.float32) + dot(att[...], w[:, at])).astype(jnp.bfloat16)
        copy = pltpu.make_async_remote_copy(
            src_ref=osend.at[:, at],
            dst_ref=so.at[0, :, at],
            send_sem=o_s.at[c],
            recv_sem=o_r.at[c],
            device_id={"section": up},
            device_id_type=MESH,
        )
        copy.start()
        o_out.append(copy)
    backward(groups - 1, *held)

    for copy in gkv_out:
        copy.wait_recv()
    kvg[0] = kvacc[...] + kvrecv[0].astype(jnp.float32) + kvrecv[1].astype(jnp.float32)
    for copy in kv_out[0] + kv_out[1] + gkv_out:
        copy.wait_send()
    for copy in g_out + o_out:
        copy.wait()


def solution(mesh):
    n_seq, n_sec = mesh.shape["seq"], mesh.shape["section"]

    def per_device(x, kv, w, mask, cot):
        _, rows, hid = x.shape
        kvw = kv.shape[-1]
        groups = kvw // HD
        bf, f32 = jnp.bfloat16, jnp.float32
        dma = pltpu.SemaphoreType.DMA
        vmem = pl.BlockSpec(memory_space=pltpu.VMEM)
        hbm = pl.BlockSpec(memory_space=pl.ANY)
        return pl.pallas_call(
            functools.partial(kernel, n_seq, n_sec),
            out_shape=(
                jax.ShapeDtypeStruct((1, rows, hid), bf),
                jax.ShapeDtypeStruct((1, rows, hid), bf),
                jax.ShapeDtypeStruct((1, 2, rows, kvw), f32),
            ),
            in_specs=[hbm, hbm, hbm, pl.BlockSpec(memory_space=pltpu.SMEM), hbm],
            out_specs=(vmem, vmem, vmem),
            scratch_shapes=[
                pltpu.VMEM((rows, hid), bf),
                pltpu.VMEM((rows, hid), bf),
                pltpu.VMEM((hid, hid), bf),
                pltpu.VMEM((2, rows, kvw), bf),
                pltpu.VMEM((2, 2, rows, kvw), bf),
                pltpu.VMEM((rows, hid), bf),
                pltpu.VMEM((rows, hid), bf),
                pltpu.VMEM((rows, hid), bf),
                pltpu.VMEM((rows, hid), bf),
                pltpu.VMEM((2, 2, rows, kvw), bf),
                pltpu.VMEM((2, 2, rows, kvw), bf),
                pltpu.VMEM((2, rows, kvw), f32),
                dma((3,)),
                dma((groups,)),
                dma((2, groups)),
                dma((2, groups)),
                dma((2, groups)),
                dma((2, groups)),
                dma((groups,)),
                dma((groups,)),
                dma((groups,)),
                dma((groups,)),
            ],
            compiler_params=pltpu.CompilerParams(
                collective_id=0, has_side_effects=True, vmem_limit_bytes=60 * 1024 * 1024
            ),
        )(x, kv, w, mask, cot)

    return jax.shard_map(
        per_device,
        mesh=mesh,
        in_specs=(
            P("section", "seq", None),
            P("section", None, "seq", None),
            P("section", None, None),
            P("section", None, None),
            P("section", "seq", None),
        ),
        out_specs=(
            P("section", "seq", None),
            P("section", "seq", None),
            P("section", None, "seq", None),
        ),
        check_vma=False,
    )
```

```python
import functools

import jax
import jax.numpy as jnp
from jax import lax
from jax.experimental import pallas as pl
from jax.experimental.pallas import tpu as pltpu
from jax.sharding import PartitionSpec as P

HD = 128
MESH = pl.DeviceIdType.MESH
NT = (((1,), (1,)), ((), ()))
NN = (((1,), (0,)), ((), ()))
EVEN_AFTER = 1
ARRIVE = 0
ORDER = [(step, int(g)) for step, g in zip("ffffobobobob", "012300112233")]


def dot(a, b, dims=NN):
    return lax.dot_general(a, b, dims, preferred_element_type=jnp.float32)


def cols(start, count=1):
    return pl.ds(start * HD, count * HD)


def kernel(
    n_seq, n_sec,
    x_hbm, kv_hbm, w_hbm, mask, cot_hbm,
    so, sg, kvg,
    x, cot, w, kv, kvin, datt, att, gsend, osend, kvsend, kvrecv, kvacc,
    lsem, wsem, kv_s, kv_r, gkv_s, gkv_r, g_s, g_r, o_s, o_r,
):
    seq, sec = lax.axis_index("seq"), lax.axis_index("section")
    groups = kv.shape[2] // HD
    heads = x.shape[1] // HD // groups
    tiles = x.shape[1] // HD
    width = heads * HD
    scale = HD ** -0.5
    to_exp2 = scale * 1.4426950408889634
    even = lax.rem(seq, 2) == 0
    odd = lax.rem(seq, 2) == 1
    has_next = seq + 2 < n_seq
    has_prev = seq >= 2
    mate = seq + 1 - 2 * lax.rem(seq, 2)
    ahead = lax.rem(seq + 2, n_seq)
    behind = lax.rem(seq + n_seq - 2, n_seq)
    before = lax.rem(seq + n_seq - 1, n_seq)
    cross = lax.rem(seq + n_seq + 2 * lax.rem(seq, 2) - 1, n_seq)
    has_cross = (even & has_prev) | (odd & has_next)
    up, down = lax.rem(sec + 1, n_sec), lax.rem(sec + n_sec - 1, n_sec)

    loads = [
        pltpu.make_async_copy(kv_hbm.at[0], kv, lsem.at[0]),
        pltpu.make_async_copy(cot_hbm.at[0], cot, lsem.at[1]),
        pltpu.make_async_copy(x_hbm.at[0], x, lsem.at[2]),
    ]
    wloads = [
        pltpu.make_async_copy(w_hbm.at[0, cols(g * heads, heads)], w.at[cols(g * heads, heads)], wsem.at[g])
        for g in range(groups)
    ]
    for copy in loads + wloads:
        copy.start()

    barrier = pltpu.get_barrier_semaphore()

    def greet(peer):
        pl.semaphore_signal(barrier, inc=1, device_id={"seq": peer}, device_id_type=MESH)

    greet(mate)
    for there, peer in ((has_next, ahead), (has_prev, behind), (has_cross, cross)):
        pl.when(there)(functools.partial(greet, peer))
    for peer in (up, down):
        pl.semaphore_signal(barrier, inc=1, device_id={"section": peer}, device_id_type=MESH)
    one = [there.astype(jnp.int32) for there in (has_next, has_prev, has_cross)]
    pl.semaphore_wait(barrier, 3 + one[0] + one[1] + one[2])

    def kv_copy(d, g, src, peer):
        return pltpu.make_async_remote_copy(
            src_ref=src,
            dst_ref=kvin.at[d, :, :, cols(g)],
            send_sem=kv_s.at[d, g],
            recv_sem=kv_r.at[d, g],
            device_id={"seq": peer},
            device_id_type=MESH,
        )

    direct = [kv_copy(0, g, kv_hbm.at[0, :, :, cols(g)], mate) for g in range(groups)]
    relay = [kv_copy(0, g, kvin.at[1, :, :, cols(g)], mate) for g in range(groups)]
    hop = [kv_copy(1, g, kv_hbm.at[0, :, :, cols(g)], ahead) for g in range(groups)]

    @pl.when(odd & has_next)
    def _():
        for copy in hop:
            copy.start()

    @pl.when(even)
    def _():
        for copy in direct:
            copy.start()

    @pl.when(jnp.logical_not(has_prev))
    def _():
        kvin[1] = jnp.zeros(kvin.shape[1:], kvin.dtype)

    @pl.when(seq == 0)
    def _():
        kvin[0] = jnp.zeros(kvin.shape[1:], kvin.dtype)

    @pl.when(jnp.logical_not(has_next))
    def _():
        kvrecv[1] = jnp.zeros(kvrecv.shape[1:], kvrecv.dtype)

    @pl.when(odd & jnp.logical_not(has_next))
    def _():
        kvrecv[0] = jnp.zeros(kvrecv.shape[1:], kvrecv.dtype)

    loads[1].wait()
    cot_v = cot[...]
    for g in range(groups):
        wloads[g].wait()
        for a in range(g * heads, (g + 1) * heads):
            for b in range(tiles):
                keep = mask[0, a, b].astype(jnp.float32).astype(jnp.bfloat16)
                w[cols(a), cols(b)] = w[cols(a), cols(b)] * keep
        full = dot(w[cols(g * heads, heads), :], cot_v, NT).astype(jnp.bfloat16)
        for h in range(heads):
            datt[:, cols(g * heads + h)] = full[h * HD : (h + 1) * HD]
        if g == EVEN_AFTER:
            @pl.when(even & has_next)
            def _():
                for copy in hop:
                    copy.start()

    loads[0].wait()
    loads[2].wait()
    key = lax.broadcasted_iota(jnp.int32, (HD, width), 0)
    tok = lax.broadcasted_iota(jnp.int32, (HD, width), 1) % HD
    own = key <= tok
    low = jnp.float32(-1e30)
    bias1 = jnp.where(seq >= 1, jnp.float32(0), low)
    bias2 = jnp.where(seq >= 2, jnp.float32(0), low)
    zero = jnp.zeros((HD, width), jnp.bfloat16)

    def split(block, prev):
        return jnp.concatenate(
            [jnp.where(own, block, zero), prev, jnp.where(own, zero, block)], axis=0
        )

    g_out, gkv_out = [], []

    arrived = []

    def arrive(upto):
        for g in range(len(arrived), max(upto + 1, ARRIVE)):
            arrived.append(g)

            @pl.when(has_prev)
            def _():
                hop[g].wait_recv()

            @pl.when(odd & has_prev)
            def _():
                relay[g].start()

    def forward(g):
        arrive(g)

        @pl.when(even & has_prev | odd)
        def _():
            direct[g].wait_recv()

        ks = jnp.concatenate([kv[0, :, cols(g)], kvin[0, 0, :, cols(g)], kvin[1, 0, :, cols(g)]], axis=0)
        vs = jnp.concatenate([kv[1, :, cols(g)], kvin[0, 1, :, cols(g)], kvin[1, 1, :, cols(g)]], axis=0)
        qs = jnp.concatenate([x[:, cols(g * heads + h)] for h in range(heads)], axis=0)
        s = dot(ks, qs, NT)
        sc = jnp.where(own, s[:HD], s[2 * HD :] + bias2)
        s1 = s[HD : 2 * HD] + bias1
        top = jnp.maximum(jnp.max(sc, axis=0, keepdims=True), jnp.max(s1, axis=0, keepdims=True))
        ec = jnp.exp2((sc - top) * to_exp2)
        e1 = jnp.exp2((s1 - top) * to_exp2)
        inv = 1.0 / (jnp.sum(ec, axis=0, keepdims=True) + jnp.sum(e1, axis=0, keepdims=True))
        pc, p1 = ec * inv, e1 * inv
        pb = split(pc.astype(jnp.bfloat16), p1.astype(jnp.bfloat16))
        out_t = dot(vs.T, pb).astype(jnp.bfloat16)
        for h in range(heads):
            att[:, cols(g * heads + h)] = out_t[:, h * HD : (h + 1) * HD].T
        return ks, vs, qs, pc, p1, pb

    def backward(g, ks, vs, qs, pc, p1, pb):
        dt = datt[:, cols(g * heads, heads)]
        dp = dot(vs, dt)
        dc, d1 = jnp.where(own, dp[:HD], dp[2 * HD :]), dp[HD : 2 * HD]
        row = jnp.sum(pc * dc, axis=0, keepdims=True) + jnp.sum(p1 * d1, axis=0, keepdims=True)
        ds = split((pc * (dc - row)).astype(jnp.bfloat16), (p1 * (d1 - row)).astype(jnp.bfloat16))
        dq_t = dot(ks.T, ds) * scale
        for h in range(heads):
            at = cols(g * heads + h)
            gsend[:, at] = (cot[:, at].astype(jnp.float32) + dq_t[:, h * HD : (h + 1) * HD].T).astype(jnp.bfloat16)
        copy = pltpu.make_async_remote_copy(
            src_ref=gsend.at[:, cols(g * heads, heads)],
            dst_ref=sg.at[0, :, cols(g * heads, heads)],
            send_sem=g_s.at[g],
            recv_sem=g_r.at[g],
            device_id={"section": down},
            device_id_type=MESH,
        )
        copy.start()
        g_out.append(copy)
        both = [dot(ds, qs) * scale, dot(pb, dt, NT)]
        for i in range(2):
            kvacc[i, :, cols(g)] = both[i][:HD]
            for d in range(2):
                kvsend[d, i, :, cols(g)] = both[i][(d + 1) * HD : (d + 2) * HD].astype(jnp.bfloat16)
        pair = [
            pltpu.make_async_remote_copy(
                src_ref=kvsend.at[d, :, :, cols(g)],
                dst_ref=kvrecv.at[d, :, :, cols(g)],
                send_sem=gkv_s.at[d, g],
                recv_sem=gkv_r.at[d, g],
                device_id={"seq": (before, behind)[d]},
                device_id_type=MESH,
            )
            for d in range(2)
        ]
        pl.when(odd | has_prev)(pair[0].start)
        pl.when(has_prev)(pair[1].start)
        gkv_out.append(pair)

    def project(c):
        at = cols(c * heads, heads)
        osend[:, at] = (x[:, at].astype(jnp.float32) + dot(att[...], w[:, at])).astype(jnp.bfloat16)
        copy = pltpu.make_async_remote_copy(
            src_ref=osend.at[:, at],
            dst_ref=so.at[0, :, at],
            send_sem=o_s.at[c],
            recv_sem=o_r.at[c],
            device_id={"section": up},
            device_id_type=MESH,
        )
        copy.start()
        o_out.append(copy)

    o_out, held = [], {}
    for step, g in ORDER:
        if step == "f":
            held[g] = forward(g)
        elif step == "b":
            backward(g, *held.pop(g))
        else:
            project(g)

    @pl.when(even | has_next)
    def _():
        for pair in gkv_out:
            pair[0].wait_recv()

    @pl.when(has_next)
    def _():
        for pair in gkv_out:
            pair[1].wait_recv()

    kvg[0] = kvacc[...] + kvrecv[0].astype(jnp.float32) + kvrecv[1].astype(jnp.float32)

    @pl.when(even | has_prev)
    def _():
        for copy in direct:
            copy.wait_send()

    @pl.when(has_next)
    def _():
        for copy in hop:
            copy.wait_send()

    @pl.when(odd | has_prev)
    def _():
        for pair in gkv_out:
            pair[0].wait_send()

    @pl.when(has_prev)
    def _():
        for pair in gkv_out:
            pair[1].wait_send()

    for copy in g_out + o_out:
        copy.wait()


def store(a, b, c, a_out, b_out, c_out, sem):
    copies = [
        pltpu.make_async_copy(src, dst, sem.at[i])
        for i, (src, dst) in enumerate([(a, a_out), (b, b_out), (c, c_out)])
    ]
    for copy in copies:
        copy.start()
    for copy in copies:
        copy.wait()


def solution(mesh):
    n_seq, n_sec = mesh.shape["seq"], mesh.shape["section"]

    def per_device(x, kv, w, mask, cot):
        _, rows, hid = x.shape
        kvw = kv.shape[-1]
        groups = kvw // HD
        bf, f32 = jnp.bfloat16, jnp.float32
        dma = pltpu.SemaphoreType.DMA
        vmem = pl.BlockSpec(memory_space=pltpu.VMEM)
        hbm = pl.BlockSpec(memory_space=pl.ANY)
        outs = pl.pallas_call(
            functools.partial(kernel, n_seq, n_sec),
            out_shape=(
                pltpu.VMEM((1, rows, hid), bf),
                pltpu.VMEM((1, rows, hid), bf),
                pltpu.VMEM((1, 2, rows, kvw), f32),
            ),
            in_specs=[hbm, hbm, hbm, pl.BlockSpec(memory_space=pltpu.SMEM), hbm],
            out_specs=(vmem, vmem, vmem),
            scratch_shapes=[
                pltpu.VMEM((rows, hid), bf),
                pltpu.VMEM((rows, hid), bf),
                pltpu.VMEM((hid, hid), bf),
                pltpu.VMEM((2, rows, kvw), bf),
                pltpu.VMEM((2, 2, rows, kvw), bf),
                pltpu.VMEM((rows, hid), bf),
                pltpu.VMEM((rows, hid), bf),
                pltpu.VMEM((rows, hid), bf),
                pltpu.VMEM((rows, hid), bf),
                pltpu.VMEM((2, 2, rows, kvw), bf),
                pltpu.VMEM((2, 2, rows, kvw), bf),
                pltpu.VMEM((2, rows, kvw), f32),
                dma((3,)),
                dma((groups,)),
                dma((2, groups)),
                dma((2, groups)),
                dma((2, groups)),
                dma((2, groups)),
                dma((groups,)),
                dma((groups,)),
                dma((groups,)),
                dma((groups,)),
            ],
            compiler_params=pltpu.CompilerParams(
                collective_id=0, has_side_effects=True, vmem_limit_bytes=60 * 1024 * 1024
            ),
        )(x, kv, w, mask, cot)
        return pl.pallas_call(
            store,
            out_shape=tuple(jax.ShapeDtypeStruct(o.shape, o.dtype) for o in outs),
            in_specs=[hbm] * 3,
            out_specs=(hbm,) * 3,
            scratch_shapes=[dma((3,))],
        )(*(pltpu.with_memory_space_constraint(o, pltpu.VMEM) for o in outs))

    return jax.shard_map(
        per_device,
        mesh=mesh,
        in_specs=(
            P("section", "seq", None),
            P("section", None, "seq", None),
            P("section", None, None),
            P("section", None, None),
            P("section", "seq", None),
        ),
        out_specs=(
            P("section", "seq", None),
            P("section", "seq", None),
            P("section", None, "seq", None),
        ),
        check_vma=False,
    )
```

```python
import functools

import jax
import jax.numpy as jnp
from jax import lax
from jax.experimental import pallas as pl
from jax.experimental.pallas import tpu as pltpu
from jax.sharding import PartitionSpec as P

HD = 128
MESH = pl.DeviceIdType.MESH
NT = (((1,), (1,)), ((), ()))
NN = (((1,), (0,)), ((), ()))
SLAB = 4


def steps(names, groups):
    return [(name, int(group)) for name, group in zip(names, groups)]


FIRST = steps("dde", "010")
EVEN = steps("ddfbfbfbfboooo", "23001122330123")
ODD = steps("ffffobobdobdob", "01230011222333")


def dot(a, b, dims=NN):
    return lax.dot_general(a, b, dims, preferred_element_type=jnp.float32)


def cols(start, count=1):
    return pl.ds(start * HD, count * HD)


def kernel(
    n_seq, n_sec,
    x_hbm, kv_hbm, w_hbm, mask_hbm, cot_hbm,
    so, sg, kvg,
    mask, x, cot, w, kv, kvin, datt, att, gsend, osend, kvsend, kvrecv, kvacc,
    lsem, wsem, kv_s, kv_r, gkv_s, gkv_r, g_s, g_r, o_s, o_r,
):
    seq, sec = lax.axis_index("seq"), lax.axis_index("section")
    groups = kv.shape[2] // HD
    heads = x.shape[1] // HD // groups
    tiles = x.shape[1] // HD
    width = heads * HD
    scale = HD ** -0.5
    to_exp2 = scale * 1.4426950408889634
    even = lax.rem(seq, 2) == 0
    odd = lax.rem(seq, 2) == 1
    has_next = seq + 2 < n_seq
    has_prev = seq >= 2
    mate = seq + 1 - 2 * lax.rem(seq, 2)
    ahead = lax.rem(seq + 2, n_seq)
    behind = lax.rem(seq + n_seq - 2, n_seq)
    before = lax.rem(seq + n_seq - 1, n_seq)
    cross = lax.rem(seq + n_seq + 2 * lax.rem(seq, 2) - 1, n_seq)
    has_cross = (even & has_prev) | (odd & has_next)
    up, down = lax.rem(sec + 1, n_sec), lax.rem(sec + n_sec - 1, n_sec)

    loads = [
        pltpu.make_async_copy(kv_hbm.at[0], kv, lsem.at[0]),
        pltpu.make_async_copy(cot_hbm.at[0], cot, lsem.at[1]),
        pltpu.make_async_copy(x_hbm.at[0], x, lsem.at[2]),
        pltpu.make_async_copy(mask_hbm, mask, lsem.at[3]),
    ]
    wloads = [
        pltpu.make_async_copy(w_hbm.at[0, cols(i * SLAB, SLAB)], w.at[cols(i * SLAB, SLAB)], wsem.at[i])
        for i in range(tiles // SLAB)
    ]
    for copy in loads + wloads:
        copy.start()

    barrier = pltpu.get_barrier_semaphore()

    def greet(peer):
        pl.semaphore_signal(barrier, inc=1, device_id={"seq": peer}, device_id_type=MESH)

    greet(mate)
    for there, peer in ((has_next, ahead), (has_prev, behind), (has_cross, cross)):
        pl.when(there)(functools.partial(greet, peer))
    for peer in (up, down):
        pl.semaphore_signal(barrier, inc=1, device_id={"section": peer}, device_id_type=MESH)
    one = [there.astype(jnp.int32) for there in (has_next, has_prev, has_cross)]
    pl.semaphore_wait(barrier, 3 + one[0] + one[1] + one[2])

    def kv_copy(d, g, src, peer):
        return pltpu.make_async_remote_copy(
            src_ref=src,
            dst_ref=kvin.at[d, :, :, cols(g)],
            send_sem=kv_s.at[d, g],
            recv_sem=kv_r.at[d, g],
            device_id={"seq": peer},
            device_id_type=MESH,
        )

    direct = [kv_copy(0, g, kv_hbm.at[0, :, :, cols(g)], mate) for g in range(groups)]
    relay = [kv_copy(0, g, kvin.at[1, :, :, cols(g)], mate) for g in range(groups)]
    hop = [kv_copy(1, g, kv_hbm.at[0, :, :, cols(g)], ahead) for g in range(groups)]

    @pl.when(odd & has_next)
    def _():
        for copy in hop:
            copy.start()

    @pl.when(even)
    def _():
        for copy in direct:
            copy.start()

    @pl.when(jnp.logical_not(has_prev))
    def _():
        kvin[1] = jnp.zeros(kvin.shape[1:], kvin.dtype)

    @pl.when(seq == 0)
    def _():
        kvin[0] = jnp.zeros(kvin.shape[1:], kvin.dtype)

    @pl.when(jnp.logical_not(has_next))
    def _():
        kvrecv[1] = jnp.zeros(kvrecv.shape[1:], kvrecv.dtype)

    @pl.when(odd & jnp.logical_not(has_next))
    def _():
        kvrecv[0] = jnp.zeros(kvrecv.shape[1:], kvrecv.dtype)

    loads[3].wait()
    loads[1].wait()
    pruned, landed = set(), set()

    def prune(a, c):
        if a // SLAB not in landed:
            landed.add(a // SLAB)
            wloads[a // SLAB].wait()
        if (a, c) in pruned:
            return
        pruned.add((a, c))
        for b in range(c * heads, (c + 1) * heads):
            keep = mask[0, a, b].astype(jnp.float32).astype(jnp.bfloat16)
            w[cols(a), cols(b)] = w[cols(a), cols(b)] * keep

    def attended_grad(g):
        for a in range(g * heads, (g + 1) * heads):
            for c in range(groups):
                prune(a, c)
        at = cols(g * heads, heads)
        datt[:, at] = dot(cot[...], w[at, :], NT).astype(jnp.bfloat16)

    def send_even():
        @pl.when(even & has_next)
        def _():
            for copy in hop:
                copy.start()

    key = lax.broadcasted_iota(jnp.int32, (HD, width), 0)
    tok = lax.broadcasted_iota(jnp.int32, (HD, width), 1) % HD
    own = key <= tok
    low = jnp.float32(-1e30)
    bias1 = jnp.where(seq >= 1, jnp.float32(0), low)
    bias2 = jnp.where(seq >= 2, jnp.float32(0), low)
    zero = jnp.zeros((HD, width), jnp.bfloat16)

    def split(block, prev):
        return jnp.concatenate(
            [jnp.where(own, block, zero), prev, jnp.where(own, zero, block)], axis=0
        )

    def strip(src, dst, sems, g, peer):
        at = cols(g * heads, heads)
        return pltpu.make_async_remote_copy(
            src_ref=src.at[:, at],
            dst_ref=dst.at[0, :, at],
            send_sem=sems[0].at[g],
            recv_sem=sems[1].at[g],
            device_id={"section": peer},
            device_id_type=MESH,
        )

    g_out = [strip(gsend, sg, (g_s, g_r), g, down) for g in range(groups)]
    o_out = [strip(osend, so, (o_s, o_r), g, up) for g in range(groups)]
    gkv_out = [
        [
            pltpu.make_async_remote_copy(
                src_ref=kvsend.at[d, :, :, cols(g)],
                dst_ref=kvrecv.at[d, :, :, cols(g)],
                send_sem=gkv_s.at[d, g],
                recv_sem=gkv_r.at[d, g],
                device_id={"seq": (before, behind)[d]},
                device_id_type=MESH,
            )
            for d in range(2)
        ]
        for g in range(groups)
    ]

    def forward(parity, g):
        @pl.when(has_prev)
        def _():
            hop[g].wait_recv()
            if parity:
                relay[g].start()
            else:
                direct[g].wait_recv()

        if parity:
            direct[g].wait_recv()
        ks = jnp.concatenate([kv[0, :, cols(g)], kvin[0, 0, :, cols(g)], kvin[1, 0, :, cols(g)]], axis=0)
        vs = jnp.concatenate([kv[1, :, cols(g)], kvin[0, 1, :, cols(g)], kvin[1, 1, :, cols(g)]], axis=0)
        qs = jnp.concatenate([x[:, cols(g * heads + h)] for h in range(heads)], axis=0)
        s = dot(ks, qs, NT)
        sc = jnp.where(own, s[:HD], s[2 * HD :] + bias2)
        s1 = s[HD : 2 * HD] + bias1
        top = jnp.maximum(jnp.max(sc, axis=0, keepdims=True), jnp.max(s1, axis=0, keepdims=True))
        ec = jnp.exp2((sc - top) * to_exp2)
        e1 = jnp.exp2((s1 - top) * to_exp2)
        inv = 1.0 / (jnp.sum(ec, axis=0, keepdims=True) + jnp.sum(e1, axis=0, keepdims=True))
        pc, p1 = ec * inv, e1 * inv
        pb = split(pc.astype(jnp.bfloat16), p1.astype(jnp.bfloat16))
        out_t = dot(vs.T, pb).astype(jnp.bfloat16)
        for h in range(heads):
            att[:, cols(g * heads + h)] = out_t[:, h * HD : (h + 1) * HD].T
        return ks, vs, qs, pc, p1, pb

    def backward(parity, g, ks, vs, qs, pc, p1, pb):
        dt = jnp.concatenate([datt[:, cols(g * heads + h)] for h in range(heads)], axis=0)
        dp = dot(vs, dt, NT)
        dc, d1 = jnp.where(own, dp[:HD], dp[2 * HD :]), dp[HD : 2 * HD]
        row = jnp.sum(pc * dc, axis=0, keepdims=True) + jnp.sum(p1 * d1, axis=0, keepdims=True)
        ds = split((pc * (dc - row)).astype(jnp.bfloat16), (p1 * (d1 - row)).astype(jnp.bfloat16))
        dq_t = dot(ks.T, ds) * scale
        for h in range(heads):
            at = cols(g * heads + h)
            gsend[:, at] = (cot[:, at].astype(jnp.float32) + dq_t[:, h * HD : (h + 1) * HD].T).astype(jnp.bfloat16)
        g_out[g].start()
        both = [dot(ds, qs) * scale, dot(pb, dt)]
        for i in range(2):
            kvacc[i, :, cols(g)] = both[i][:HD]
            for d in range(2):
                kvsend[d, i, :, cols(g)] = both[i][(d + 1) * HD : (d + 2) * HD].astype(jnp.bfloat16)
        if parity:
            gkv_out[g][0].start()
        else:
            pl.when(has_prev)(gkv_out[g][0].start)
        pl.when(has_prev)(gkv_out[g][1].start)

    def project(c):
        for a in range(tiles):
            prune(a, c)
        at = cols(c * heads, heads)
        osend[:, at] = (x[:, at].astype(jnp.float32) + dot(att[...], w[:, at])).astype(jnp.bfloat16)
        o_out[c].start()

    def run(parity, order):
        held = {}
        for step, g in order:
            if step == "d":
                attended_grad(g)
            elif step == "e":
                send_even()
            elif step == "f":
                held[g] = forward(parity, g)
            elif step == "b":
                backward(parity, g, *held.pop(g))
            else:
                project(g)

    run(None, FIRST)
    for i, copy in enumerate(wloads):
        if i not in landed:
            copy.wait()
            landed.add(i)
    loads[0].wait()
    loads[2].wait()
    shared = set(pruned)

    @pl.when(even)
    def _():
        run(0, EVEN)

    pruned.clear()
    pruned.update(shared)

    @pl.when(odd)
    def _():
        run(1, ODD)

    for g in range(groups):
        at = cols(g)
        pl.when(even | has_next)(gkv_out[g][0].wait_recv)
        pl.when(has_next)(gkv_out[g][1].wait_recv)
        kvg[0, :, :, at] = (
            kvacc[:, :, at] + kvrecv[0, :, :, at].astype(jnp.float32) + kvrecv[1, :, :, at].astype(jnp.float32)
        )

    @pl.when(even | has_prev)
    def _():
        for copy in direct:
            copy.wait_send()

    @pl.when(has_next)
    def _():
        for copy in hop:
            copy.wait_send()

    @pl.when(odd | has_prev)
    def _():
        for pair in gkv_out:
            pair[0].wait_send()

    @pl.when(has_prev)
    def _():
        for pair in gkv_out:
            pair[1].wait_send()

    for copy in g_out + o_out:
        copy.wait()


def store(a, b, c, a_out, b_out, c_out, sem):
    copies = [
        pltpu.make_async_copy(src, dst, sem.at[i])
        for i, (src, dst) in enumerate([(a, a_out), (b, b_out), (c, c_out)])
    ]
    for copy in copies:
        copy.start()
    for copy in copies:
        copy.wait()


def solution(mesh):
    n_seq, n_sec = mesh.shape["seq"], mesh.shape["section"]

    def per_device(x, kv, w, mask, cot):
        _, rows, hid = x.shape
        kvw = kv.shape[-1]
        groups = kvw // HD
        bf, f32 = jnp.bfloat16, jnp.float32
        dma = pltpu.SemaphoreType.DMA
        vmem = pl.BlockSpec(memory_space=pltpu.VMEM)
        hbm = pl.BlockSpec(memory_space=pl.ANY)
        outs = pl.pallas_call(
            functools.partial(kernel, n_seq, n_sec),
            out_shape=(
                pltpu.VMEM((1, rows, hid), bf),
                pltpu.VMEM((1, rows, hid), bf),
                pltpu.VMEM((1, 2, rows, kvw), f32),
            ),
            in_specs=[hbm] * 5,
            out_specs=(vmem, vmem, vmem),
            scratch_shapes=[
                pltpu.SMEM(mask.shape, mask.dtype),
                pltpu.VMEM((rows, hid), bf),
                pltpu.VMEM((rows, hid), bf),
                pltpu.VMEM((hid, hid), bf),
                pltpu.VMEM((2, rows, kvw), bf),
                pltpu.VMEM((2, 2, rows, kvw), bf),
                pltpu.VMEM((rows, hid), bf),
                pltpu.VMEM((rows, hid), bf),
                pltpu.VMEM((rows, hid), bf),
                pltpu.VMEM((rows, hid), bf),
                pltpu.VMEM((2, 2, rows, kvw), bf),
                pltpu.VMEM((2, 2, rows, kvw), bf),
                pltpu.VMEM((2, rows, kvw), f32),
                dma((4,)),
                dma((hid // HD // SLAB,)),
                dma((2, groups)),
                dma((2, groups)),
                dma((2, groups)),
                dma((2, groups)),
                dma((groups,)),
                dma((groups,)),
                dma((groups,)),
                dma((groups,)),
            ],
            compiler_params=pltpu.CompilerParams(
                collective_id=0, has_side_effects=True, vmem_limit_bytes=60 * 1024 * 1024
            ),
        )(x, kv, w, mask, cot)
        return pl.pallas_call(
            store,
            out_shape=tuple(jax.ShapeDtypeStruct(o.shape, o.dtype) for o in outs),
            in_specs=[hbm] * 3,
            out_specs=(hbm,) * 3,
            scratch_shapes=[dma((3,))],
        )(*(pltpu.with_memory_space_constraint(o, pltpu.VMEM) for o in outs))

    return jax.shard_map(
        per_device,
        mesh=mesh,
        in_specs=(
            P("section", "seq", None),
            P("section", None, "seq", None),
            P("section", None, None),
            P("section", None, None),
            P("section", "seq", None),
        ),
        out_specs=(
            P("section", "seq", None),
            P("section", "seq", None),
            P("section", None, "seq", None),
        ),
        check_vma=False,
    )
```

```python
import functools

import jax
import jax.numpy as jnp
from jax import lax
from jax.experimental import pallas as pl
from jax.experimental.pallas import tpu as pltpu
from jax.sharding import PartitionSpec as P

HD = 128
MESH = pl.DeviceIdType.MESH
NT = (((1,), (1,)), ((), ()))
NN = (((1,), (0,)), ((), ()))
SLAB = 4


def steps(names, groups):
    return [(name, int(group)) for name, group in zip(names, groups)]


ROW = 24
PARTS = 4
FIRST = steps("dde", "010")
EVEN = steps("ddfbfbfbfboooo", "23001122330123")
ODD = steps("ffffobobdobdob", "01230011222333")


def dot(a, b, dims=NN):
    return lax.dot_general(a, b, dims, preferred_element_type=jnp.float32)


def cols(start, count=1):
    return pl.ds(start * HD, count * HD)


def kernel(
    n_seq, n_sec,
    x_hbm, kv_hbm, w_hbm, mask_hbm, cot_hbm,
    so, sg, kvg,
    mask, x, cot, w, kv, kvin, datt, att, gsend, osend, kvsend, kvrecv, kvacc,
    lsem, wsem, kv_s, kv_r, gkv_s, gkv_r, g_s, g_r, o_s, o_r,
):
    seq, sec = lax.axis_index("seq"), lax.axis_index("section")
    groups = kv.shape[2] // HD
    heads = x.shape[1] // HD // groups
    tiles = x.shape[1] // HD
    width = heads * HD
    scale = HD ** -0.5
    to_exp2 = scale * 1.4426950408889634
    even = lax.rem(seq, 2) == 0
    odd = lax.rem(seq, 2) == 1
    has_next = seq + 2 < n_seq
    has_prev = seq >= 2
    waits = (lax.rem(seq, ROW) < 2) & has_prev
    goes = jnp.logical_not(waits)
    mate = seq + 1 - 2 * lax.rem(seq, 2)
    ahead = lax.rem(seq + 2, n_seq)
    behind = lax.rem(seq + n_seq - 2, n_seq)
    before = lax.rem(seq + n_seq - 1, n_seq)
    cross = lax.rem(seq + n_seq + 2 * lax.rem(seq, 2) - 1, n_seq)
    has_cross = (even & has_prev) | (odd & has_next)
    up, down = lax.rem(sec + 1, n_sec), lax.rem(sec + n_sec - 1, n_sec)

    loads = [
        pltpu.make_async_copy(kv_hbm.at[0], kv, lsem.at[0]),
        pltpu.make_async_copy(cot_hbm.at[0], cot, lsem.at[1]),
        pltpu.make_async_copy(x_hbm.at[0], x, lsem.at[2]),
        pltpu.make_async_copy(mask_hbm, mask, lsem.at[3]),
    ]
    wloads = [
        pltpu.make_async_copy(w_hbm.at[0, cols(i * SLAB, SLAB)], w.at[cols(i * SLAB, SLAB)], wsem.at[i])
        for i in range(tiles // SLAB)
    ]
    for copy in loads + wloads:
        copy.start()

    barrier = pltpu.get_barrier_semaphore()

    def greet(peer):
        pl.semaphore_signal(barrier, inc=1, device_id={"seq": peer}, device_id_type=MESH)

    greet(mate)
    for there, peer in ((has_next, ahead), (has_prev, behind), (has_cross, cross)):
        pl.when(there)(functools.partial(greet, peer))
    for peer in (up, down):
        pl.semaphore_signal(barrier, inc=1, device_id={"section": peer}, device_id_type=MESH)
    loads[3].wait()
    loads[1].wait()
    pruned, landed = set(), set()

    def prune(a, c):
        if a // SLAB not in landed:
            landed.add(a // SLAB)
            wloads[a // SLAB].wait()
        if (a, c) in pruned:
            return
        pruned.add((a, c))
        for b in range(c * heads, (c + 1) * heads):
            keep = mask[0, a, b].astype(jnp.float32).astype(jnp.bfloat16)
            w[cols(a), cols(b)] = w[cols(a), cols(b)] * keep

    def attended_grad(g, keep_set=None):
        for a in range(g * heads, (g + 1) * heads):
            for c in range(groups):
                prune(a, c)
        if keep_set is not None:
            pruned.clear()
            pruned.update(keep_set)
        at = cols(g * heads, heads)
        datt[:, at] = dot(cot[...], w[at, :], NT).astype(jnp.bfloat16)

    def land():
        for i, copy in enumerate(wloads):
            if i not in landed:
                landed.add(i)
                copy.wait()

    @pl.when(waits)
    def _():
        for g in range(groups):
            attended_grad(g)

    pruned.clear()
    landed.clear()
    one = [there.astype(jnp.int32) for there in (has_next, has_prev, has_cross)]
    pl.semaphore_wait(barrier, 3 + one[0] + one[1] + one[2])

    def kv_copy(d, g, src, peer):
        return pltpu.make_async_remote_copy(
            src_ref=src,
            dst_ref=kvin.at[d, :, :, cols(g)],
            send_sem=kv_s.at[d, g],
            recv_sem=kv_r.at[d, g],
            device_id={"seq": peer},
            device_id_type=MESH,
        )

    direct = [kv_copy(0, g, kv_hbm.at[0, :, :, cols(g)], mate) for g in range(groups)]
    relay = [kv_copy(0, g, kvin.at[1, :, :, cols(g)], mate) for g in range(groups)]
    hop = [kv_copy(1, g, kv_hbm.at[0, :, :, cols(g)], ahead) for g in range(groups)]

    @pl.when(odd & has_next)
    def _():
        for copy in hop:
            copy.start()

    @pl.when(even)
    def _():
        for copy in direct:
            copy.start()

    @pl.when(jnp.logical_not(has_prev))
    def _():
        kvin[1] = jnp.zeros(kvin.shape[1:], kvin.dtype)

    @pl.when(seq == 0)
    def _():
        kvin[0] = jnp.zeros(kvin.shape[1:], kvin.dtype)

    @pl.when(jnp.logical_not(has_next))
    def _():
        kvrecv[1] = jnp.zeros(kvrecv.shape[1:], kvrecv.dtype)

    @pl.when(odd & jnp.logical_not(has_next))
    def _():
        kvrecv[0] = jnp.zeros(kvrecv.shape[1:], kvrecv.dtype)

    def send_even():
        @pl.when(even & has_next)
        def _():
            for copy in hop:
                copy.start()

    key = lax.broadcasted_iota(jnp.int32, (HD, width), 0)
    tok = lax.broadcasted_iota(jnp.int32, (HD, width), 1) % HD
    own = key <= tok
    low = jnp.float32(-1e30)
    bias1 = jnp.where(seq >= 1, jnp.float32(0), low)
    bias2 = jnp.where(seq >= 2, jnp.float32(0), low)
    zero = jnp.zeros((HD, width), jnp.bfloat16)

    def split(block, prev):
        return jnp.concatenate(
            [jnp.where(own, block, zero), prev, jnp.where(own, zero, block)], axis=0
        )

    def strip(src, dst, sems, g, peer):
        at = cols(g * heads, heads)
        return pltpu.make_async_remote_copy(
            src_ref=src.at[:, at],
            dst_ref=dst.at[0, :, at],
            send_sem=sems[0].at[g],
            recv_sem=sems[1].at[g],
            device_id={"section": peer},
            device_id_type=MESH,
        )

    g_out = [strip(gsend, sg, (g_s, g_r), g, down) for g in range(groups)]
    o_out = [strip(osend, so, (o_s, o_r), g, up) for g in range(groups)]
    gkv_out = [
        [
            pltpu.make_async_remote_copy(
                src_ref=kvsend.at[d, :, :, cols(g)],
                dst_ref=kvrecv.at[d, :, :, cols(g)],
                send_sem=gkv_s.at[d, g],
                recv_sem=gkv_r.at[d, g],
                device_id={"seq": (before, behind)[d]},
                device_id_type=MESH,
            )
            for d in range(2)
        ]
        for g in range(groups)
    ]

    def forward(parity, g):
        @pl.when(has_prev)
        def _():
            hop[g].wait_recv()
            if parity:
                relay[g].start()
            else:
                direct[g].wait_recv()

        if parity:
            direct[g].wait_recv()
        ks = jnp.concatenate([kv[0, :, cols(g)], kvin[0, 0, :, cols(g)], kvin[1, 0, :, cols(g)]], axis=0)
        vs = jnp.concatenate([kv[1, :, cols(g)], kvin[0, 1, :, cols(g)], kvin[1, 1, :, cols(g)]], axis=0)
        qs = jnp.concatenate([x[:, cols(g * heads + h)] for h in range(heads)], axis=0)
        s = dot(ks, qs, NT)
        sc = jnp.where(own, s[:HD], s[2 * HD :] + bias2)
        s1 = s[HD : 2 * HD] + bias1
        top = jnp.maximum(jnp.max(sc, axis=0, keepdims=True), jnp.max(s1, axis=0, keepdims=True))
        ec = jnp.exp2((sc - top) * to_exp2)
        e1 = jnp.exp2((s1 - top) * to_exp2)
        inv = 1.0 / (jnp.sum(ec, axis=0, keepdims=True) + jnp.sum(e1, axis=0, keepdims=True))
        pc, p1 = ec * inv, e1 * inv
        pb = split(pc.astype(jnp.bfloat16), p1.astype(jnp.bfloat16))
        out_t = dot(vs.T, pb).astype(jnp.bfloat16)
        for h in range(heads):
            att[:, cols(g * heads + h)] = out_t[:, h * HD : (h + 1) * HD].T
        return ks, vs, qs, pc, p1, pb

    def backward(parity, g, ks, vs, qs, pc, p1, pb):
        dt = jnp.concatenate([datt[:, cols(g * heads + h)] for h in range(heads)], axis=0)
        dp = dot(vs, dt, NT)
        dc, d1 = jnp.where(own, dp[:HD], dp[2 * HD :]), dp[HD : 2 * HD]
        row = jnp.sum(pc * dc, axis=0, keepdims=True) + jnp.sum(p1 * d1, axis=0, keepdims=True)
        ds = split((pc * (dc - row)).astype(jnp.bfloat16), (p1 * (d1 - row)).astype(jnp.bfloat16))
        dq_t = dot(ks.T, ds) * scale
        for h in range(heads):
            at = cols(g * heads + h)
            gsend[:, at] = (cot[:, at].astype(jnp.float32) + dq_t[:, h * HD : (h + 1) * HD].T).astype(jnp.bfloat16)
        g_out[g].start()
        both = [dot(ds, qs) * scale, dot(pb, dt)]
        for i in range(2):
            kvacc[i, :, cols(g)] = both[i][:HD]
            for d in range(2):
                kvsend[d, i, :, cols(g)] = both[i][(d + 1) * HD : (d + 2) * HD].astype(jnp.bfloat16)
        if parity:
            gkv_out[g][0].start()
        else:
            pl.when(has_prev)(gkv_out[g][0].start)
        pl.when(has_prev)(gkv_out[g][1].start)

    def project(c):
        for a in range(tiles):
            prune(a, c)
        at = cols(c * heads, heads)
        osend[:, at] = (x[:, at].astype(jnp.float32) + dot(att[...], w[:, at])).astype(jnp.bfloat16)
        o_out[c].start()

    def run(parity, order):
        held = {}
        for step, g in order:
            if step == "d" and parity is None:
                attended_grad(g)
            elif step == "d":
                pl.when(goes)(functools.partial(attended_grad, g, set(pruned)))
            elif step == "e":
                send_even()
            elif step == "f":
                held[g] = forward(parity, g)
            elif step == "b":
                backward(parity, g, *held.pop(g))
            else:
                project(g)

    @pl.when(goes)
    def _():
        run(None, FIRST)
        land()

    pl.when(waits)(send_even)
    loads[0].wait()
    loads[2].wait()
    shared = set(pruned)

    @pl.when(even)
    def _():
        run(0, EVEN)

    pruned.clear()
    pruned.update(shared)

    @pl.when(odd)
    def _():
        run(1, ODD)

    for g in range(groups):
        at = cols(g)
        pl.when(even | has_next)(gkv_out[g][0].wait_recv)
        pl.when(has_next)(gkv_out[g][1].wait_recv)
        kvg[0, :, :, at] = (
            kvacc[:, :, at] + kvrecv[0, :, :, at].astype(jnp.float32) + kvrecv[1, :, :, at].astype(jnp.float32)
        )

    @pl.when(even | has_prev)
    def _():
        for copy in direct:
            copy.wait_send()

    @pl.when(has_next)
    def _():
        for copy in hop:
            copy.wait_send()

    @pl.when(odd | has_prev)
    def _():
        for pair in gkv_out:
            pair[0].wait_send()

    @pl.when(has_prev)
    def _():
        for pair in gkv_out:
            pair[1].wait_send()

    for copy in g_out + o_out:
        copy.wait()


def store(a, b, c, a_out, b_out, c_out, sem):
    copies = []
    for i, (src, dst) in enumerate([(a, a_out), (b, b_out)]):
        part = src.shape[1] // PARTS
        for p in range(PARTS):
            at = pl.ds(p * part, part)
            copies.append(pltpu.make_async_copy(src.at[:, at], dst.at[:, at], sem.at[i, p]))
    part = c.shape[2] // PARTS
    for p in range(PARTS):
        at = pl.ds(p * part, part)
        copies.append(pltpu.make_async_copy(c.at[:, :, at], c_out.at[:, :, at], sem.at[2, p]))
    for copy in copies:
        copy.start()
    for copy in copies:
        copy.wait()


def solution(mesh):
    n_seq, n_sec = mesh.shape["seq"], mesh.shape["section"]

    def per_device(x, kv, w, mask, cot):
        _, rows, hid = x.shape
        kvw = kv.shape[-1]
        groups = kvw // HD
        bf, f32 = jnp.bfloat16, jnp.float32
        dma = pltpu.SemaphoreType.DMA
        vmem = pl.BlockSpec(memory_space=pltpu.VMEM)
        hbm = pl.BlockSpec(memory_space=pl.ANY)
        outs = pl.pallas_call(
            functools.partial(kernel, n_seq, n_sec),
            out_shape=(
                pltpu.VMEM((1, rows, hid), bf),
                pltpu.VMEM((1, rows, hid), bf),
                pltpu.VMEM((1, 2, rows, kvw), f32),
            ),
            in_specs=[hbm] * 5,
            out_specs=(vmem, vmem, vmem),
            scratch_shapes=[
                pltpu.SMEM(mask.shape, mask.dtype),
                pltpu.VMEM((rows, hid), bf),
                pltpu.VMEM((rows, hid), bf),
                pltpu.VMEM((hid, hid), bf),
                pltpu.VMEM((2, rows, kvw), bf),
                pltpu.VMEM((2, 2, rows, kvw), bf),
                pltpu.VMEM((rows, hid), bf),
                pltpu.VMEM((rows, hid), bf),
                pltpu.VMEM((rows, hid), bf),
                pltpu.VMEM((rows, hid), bf),
                pltpu.VMEM((2, 2, rows, kvw), bf),
                pltpu.VMEM((2, 2, rows, kvw), bf),
                pltpu.VMEM((2, rows, kvw), f32),
                dma((4,)),
                dma((hid // HD // SLAB,)),
                dma((2, groups)),
                dma((2, groups)),
                dma((2, groups)),
                dma((2, groups)),
                dma((groups,)),
                dma((groups,)),
                dma((groups,)),
                dma((groups,)),
            ],
            compiler_params=pltpu.CompilerParams(
                collective_id=0, has_side_effects=True, vmem_limit_bytes=60 * 1024 * 1024
            ),
        )(x, kv, w, mask, cot)
        return pl.pallas_call(
            store,
            out_shape=tuple(jax.ShapeDtypeStruct(o.shape, o.dtype) for o in outs),
            in_specs=[hbm] * 3,
            out_specs=(hbm,) * 3,
            scratch_shapes=[dma((3, PARTS))],
        )(*(pltpu.with_memory_space_constraint(o, pltpu.VMEM) for o in outs))

    return jax.shard_map(
        per_device,
        mesh=mesh,
        in_specs=(
            P("section", "seq", None),
            P("section", None, "seq", None),
            P("section", None, None),
            P("section", None, None),
            P("section", "seq", None),
        ),
        out_specs=(
            P("section", "seq", None),
            P("section", "seq", None),
            P("section", None, "seq", None),
        ),
        check_vma=False,
    )
```

```python
import functools

import jax
import jax.numpy as jnp
from jax import lax
from jax.experimental import pallas as pl
from jax.experimental.pallas import tpu as pltpu
from jax.sharding import PartitionSpec as P

HD = 128
MESH = pl.DeviceIdType.MESH
NT = (((1,), (1,)), ((), ()))
NN = (((1,), (0,)), ((), ()))
SLAB = 4
ARRIVE = 0
ORDER = [(step, int(g)) for step, g in zip("ddekffffobobdobdob", "010001230011222333")]


def dot(a, b, dims=NN):
    return lax.dot_general(a, b, dims, preferred_element_type=jnp.float32)


def cols(start, count=1):
    return pl.ds(start * HD, count * HD)


def kernel(
    n_seq, n_sec,
    x_hbm, kv_hbm, w_hbm, mask_hbm, cot_hbm,
    so, sg, kvg,
    mask, x, cot, w, kv, kvin, datt, att, gsend, osend, kvsend, kvrecv, kvacc,
    lsem, wsem, kv_s, kv_r, gkv_s, gkv_r, g_s, g_r, o_s, o_r,
):
    seq, sec = lax.axis_index("seq"), lax.axis_index("section")
    groups = kv.shape[2] // HD
    heads = x.shape[1] // HD // groups
    tiles = x.shape[1] // HD
    width = heads * HD
    scale = HD ** -0.5
    to_exp2 = scale * 1.4426950408889634
    even = lax.rem(seq, 2) == 0
    odd = lax.rem(seq, 2) == 1
    has_next = seq + 2 < n_seq
    has_prev = seq >= 2
    mate = seq + 1 - 2 * lax.rem(seq, 2)
    ahead = lax.rem(seq + 2, n_seq)
    behind = lax.rem(seq + n_seq - 2, n_seq)
    before = lax.rem(seq + n_seq - 1, n_seq)
    cross = lax.rem(seq + n_seq + 2 * lax.rem(seq, 2) - 1, n_seq)
    has_cross = (even & has_prev) | (odd & has_next)
    up, down = lax.rem(sec + 1, n_sec), lax.rem(sec + n_sec - 1, n_sec)

    loads = [
        pltpu.make_async_copy(kv_hbm.at[0], kv, lsem.at[0]),
        pltpu.make_async_copy(cot_hbm.at[0], cot, lsem.at[1]),
        pltpu.make_async_copy(x_hbm.at[0], x, lsem.at[2]),
        pltpu.make_async_copy(mask_hbm, mask, lsem.at[3]),
    ]
    wloads = [
        pltpu.make_async_copy(w_hbm.at[0, cols(i * SLAB, SLAB)], w.at[cols(i * SLAB, SLAB)], wsem.at[i])
        for i in range(tiles // SLAB)
    ]
    for copy in loads + wloads:
        copy.start()

    barrier = pltpu.get_barrier_semaphore()

    def greet(peer):
        pl.semaphore_signal(barrier, inc=1, device_id={"seq": peer}, device_id_type=MESH)

    greet(mate)
    for there, peer in ((has_next, ahead), (has_prev, behind), (has_cross, cross)):
        pl.when(there)(functools.partial(greet, peer))
    for peer in (up, down):
        pl.semaphore_signal(barrier, inc=1, device_id={"section": peer}, device_id_type=MESH)
    one = [there.astype(jnp.int32) for there in (has_next, has_prev, has_cross)]
    pl.semaphore_wait(barrier, 3 + one[0] + one[1] + one[2])

    def kv_copy(d, g, src, peer):
        return pltpu.make_async_remote_copy(
            src_ref=src,
            dst_ref=kvin.at[d, :, :, cols(g)],
            send_sem=kv_s.at[d, g],
            recv_sem=kv_r.at[d, g],
            device_id={"seq": peer},
            device_id_type=MESH,
        )

    direct = [kv_copy(0, g, kv_hbm.at[0, :, :, cols(g)], mate) for g in range(groups)]
    relay = [kv_copy(0, g, kvin.at[1, :, :, cols(g)], mate) for g in range(groups)]
    hop = [kv_copy(1, g, kv_hbm.at[0, :, :, cols(g)], ahead) for g in range(groups)]

    @pl.when(odd & has_next)
    def _():
        for copy in hop:
            copy.start()

    @pl.when(even)
    def _():
        for copy in direct:
            copy.start()

    @pl.when(jnp.logical_not(has_prev))
    def _():
        kvin[1] = jnp.zeros(kvin.shape[1:], kvin.dtype)

    @pl.when(seq == 0)
    def _():
        kvin[0] = jnp.zeros(kvin.shape[1:], kvin.dtype)

    @pl.when(jnp.logical_not(has_next))
    def _():
        kvrecv[1] = jnp.zeros(kvrecv.shape[1:], kvrecv.dtype)

    @pl.when(odd & jnp.logical_not(has_next))
    def _():
        kvrecv[0] = jnp.zeros(kvrecv.shape[1:], kvrecv.dtype)

    loads[3].wait()
    loads[1].wait()
    pruned, landed = set(), set()

    def prune(a, c):
        if a // SLAB not in landed:
            landed.add(a // SLAB)
            wloads[a // SLAB].wait()
        if (a, c) in pruned:
            return
        pruned.add((a, c))
        for b in range(c * heads, (c + 1) * heads):
            keep = mask[0, a, b].astype(jnp.float32).astype(jnp.bfloat16)
            w[cols(a), cols(b)] = w[cols(a), cols(b)] * keep

    def attended_grad(g):
        for a in range(g * heads, (g + 1) * heads):
            for c in range(groups):
                prune(a, c)
        at = cols(g * heads, heads)
        datt[:, at] = dot(cot[...], w[at, :], NT).astype(jnp.bfloat16)

    def send_even():
        @pl.when(even & has_next)
        def _():
            for copy in hop:
                copy.start()

    key = lax.broadcasted_iota(jnp.int32, (HD, width), 0)
    tok = lax.broadcasted_iota(jnp.int32, (HD, width), 1) % HD
    own = key <= tok
    low = jnp.float32(-1e30)
    bias1 = jnp.where(seq >= 1, jnp.float32(0), low)
    bias2 = jnp.where(seq >= 2, jnp.float32(0), low)
    zero = jnp.zeros((HD, width), jnp.bfloat16)

    def split(block, prev):
        return jnp.concatenate(
            [jnp.where(own, block, zero), prev, jnp.where(own, zero, block)], axis=0
        )

    g_out, gkv_out = [], []

    arrived = []

    def arrive(upto):
        for g in range(len(arrived), max(upto + 1, ARRIVE)):
            arrived.append(g)

            @pl.when(has_prev)
            def _():
                hop[g].wait_recv()

            @pl.when(odd & has_prev)
            def _():
                relay[g].start()

    def forward(g):
        arrive(g)

        @pl.when(even & has_prev | odd)
        def _():
            direct[g].wait_recv()

        ks = jnp.concatenate([kv[0, :, cols(g)], kvin[0, 0, :, cols(g)], kvin[1, 0, :, cols(g)]], axis=0)
        vs = jnp.concatenate([kv[1, :, cols(g)], kvin[0, 1, :, cols(g)], kvin[1, 1, :, cols(g)]], axis=0)
        qs = jnp.concatenate([x[:, cols(g * heads + h)] for h in range(heads)], axis=0)
        s = dot(ks, qs, NT)
        sc = jnp.where(own, s[:HD], s[2 * HD :] + bias2)
        s1 = s[HD : 2 * HD] + bias1
        top = jnp.maximum(jnp.max(sc, axis=0, keepdims=True), jnp.max(s1, axis=0, keepdims=True))
        ec = jnp.exp2((sc - top) * to_exp2)
        e1 = jnp.exp2((s1 - top) * to_exp2)
        inv = 1.0 / (jnp.sum(ec, axis=0, keepdims=True) + jnp.sum(e1, axis=0, keepdims=True))
        pc, p1 = ec * inv, e1 * inv
        pb = split(pc.astype(jnp.bfloat16), p1.astype(jnp.bfloat16))
        out_t = dot(vs.T, pb).astype(jnp.bfloat16)
        for h in range(heads):
            att[:, cols(g * heads + h)] = out_t[:, h * HD : (h + 1) * HD].T
        return ks, vs, qs, pc, p1, pb

    def backward(g, ks, vs, qs, pc, p1, pb):
        dt = jnp.concatenate([datt[:, cols(g * heads + h)] for h in range(heads)], axis=0)
        dp = dot(vs, dt, NT)
        dc, d1 = jnp.where(own, dp[:HD], dp[2 * HD :]), dp[HD : 2 * HD]
        row = jnp.sum(pc * dc, axis=0, keepdims=True) + jnp.sum(p1 * d1, axis=0, keepdims=True)
        ds = split((pc * (dc - row)).astype(jnp.bfloat16), (p1 * (d1 - row)).astype(jnp.bfloat16))
        dq_t = dot(ks.T, ds) * scale
        for h in range(heads):
            at = cols(g * heads + h)
            gsend[:, at] = (cot[:, at].astype(jnp.float32) + dq_t[:, h * HD : (h + 1) * HD].T).astype(jnp.bfloat16)
        copy = pltpu.make_async_remote_copy(
            src_ref=gsend.at[:, cols(g * heads, heads)],
            dst_ref=sg.at[0, :, cols(g * heads, heads)],
            send_sem=g_s.at[g],
            recv_sem=g_r.at[g],
            device_id={"section": down},
            device_id_type=MESH,
        )
        copy.start()
        g_out.append(copy)
        both = [dot(ds, qs) * scale, dot(pb, dt)]
        for i in range(2):
            kvacc[i, :, cols(g)] = both[i][:HD]
            for d in range(2):
                kvsend[d, i, :, cols(g)] = both[i][(d + 1) * HD : (d + 2) * HD].astype(jnp.bfloat16)
        pair = [
            pltpu.make_async_remote_copy(
                src_ref=kvsend.at[d, :, :, cols(g)],
                dst_ref=kvrecv.at[d, :, :, cols(g)],
                send_sem=gkv_s.at[d, g],
                recv_sem=gkv_r.at[d, g],
                device_id={"seq": (before, behind)[d]},
                device_id_type=MESH,
            )
            for d in range(2)
        ]
        pl.when(odd | has_prev)(pair[0].start)
        pl.when(has_prev)(pair[1].start)
        gkv_out.append(pair)

    def project(c):
        for a in range(tiles):
            prune(a, c)
        at = cols(c * heads, heads)
        osend[:, at] = (x[:, at].astype(jnp.float32) + dot(att[...], w[:, at])).astype(jnp.bfloat16)
        copy = pltpu.make_async_remote_copy(
            src_ref=osend.at[:, at],
            dst_ref=so.at[0, :, at],
            send_sem=o_s.at[c],
            recv_sem=o_r.at[c],
            device_id={"section": up},
            device_id_type=MESH,
        )
        copy.start()
        o_out.append(copy)

    o_out, held = [], {}
    for step, g in ORDER:
        if step == "k":
            loads[0].wait()
            loads[2].wait()
        elif step == "d":
            attended_grad(g)
        elif step == "e":
            send_even()
        elif step == "f":
            held[g] = forward(g)
        elif step == "b":
            backward(g, *held.pop(g))
        else:
            project(g)

    @pl.when(even | has_next)
    def _():
        for pair in gkv_out:
            pair[0].wait_recv()

    @pl.when(has_next)
    def _():
        for pair in gkv_out:
            pair[1].wait_recv()

    kvg[0] = kvacc[...] + kvrecv[0].astype(jnp.float32) + kvrecv[1].astype(jnp.float32)

    @pl.when(even | has_prev)
    def _():
        for copy in direct:
            copy.wait_send()

    @pl.when(has_next)
    def _():
        for copy in hop:
            copy.wait_send()

    @pl.when(odd | has_prev)
    def _():
        for pair in gkv_out:
            pair[0].wait_send()

    @pl.when(has_prev)
    def _():
        for pair in gkv_out:
            pair[1].wait_send()

    for copy in g_out + o_out:
        copy.wait()


def store(a, b, c, a_out, b_out, c_out, sem):
    copies = [
        pltpu.make_async_copy(src, dst, sem.at[i])
        for i, (src, dst) in enumerate([(a, a_out), (b, b_out), (c, c_out)])
    ]
    for copy in copies:
        copy.start()
    for copy in copies:
        copy.wait()


def solution(mesh):
    n_seq, n_sec = mesh.shape["seq"], mesh.shape["section"]

    def per_device(x, kv, w, mask, cot):
        _, rows, hid = x.shape
        kvw = kv.shape[-1]
        groups = kvw // HD
        bf, f32 = jnp.bfloat16, jnp.float32
        dma = pltpu.SemaphoreType.DMA
        vmem = pl.BlockSpec(memory_space=pltpu.VMEM)
        hbm = pl.BlockSpec(memory_space=pl.ANY)
        outs = pl.pallas_call(
            functools.partial(kernel, n_seq, n_sec),
            out_shape=(
                pltpu.VMEM((1, rows, hid), bf),
                pltpu.VMEM((1, rows, hid), bf),
                pltpu.VMEM((1, 2, rows, kvw), f32),
            ),
            in_specs=[hbm] * 5,
            out_specs=(vmem, vmem, vmem),
            scratch_shapes=[
                pltpu.SMEM(mask.shape, mask.dtype),
                pltpu.VMEM((rows, hid), bf),
                pltpu.VMEM((rows, hid), bf),
                pltpu.VMEM((hid, hid), bf),
                pltpu.VMEM((2, rows, kvw), bf),
                pltpu.VMEM((2, 2, rows, kvw), bf),
                pltpu.VMEM((rows, hid), bf),
                pltpu.VMEM((rows, hid), bf),
                pltpu.VMEM((rows, hid), bf),
                pltpu.VMEM((rows, hid), bf),
                pltpu.VMEM((2, 2, rows, kvw), bf),
                pltpu.VMEM((2, 2, rows, kvw), bf),
                pltpu.VMEM((2, rows, kvw), f32),
                dma((4,)),
                dma((hid // HD // SLAB,)),
                dma((2, groups)),
                dma((2, groups)),
                dma((2, groups)),
                dma((2, groups)),
                dma((groups,)),
                dma((groups,)),
                dma((groups,)),
                dma((groups,)),
            ],
            compiler_params=pltpu.CompilerParams(
                collective_id=0, has_side_effects=True, vmem_limit_bytes=60 * 1024 * 1024
            ),
        )(x, kv, w, mask, cot)
        return pl.pallas_call(
            store,
            out_shape=tuple(jax.ShapeDtypeStruct(o.shape, o.dtype) for o in outs),
            in_specs=[hbm] * 3,
            out_specs=(hbm,) * 3,
            scratch_shapes=[dma((3,))],
        )(*(pltpu.with_memory_space_constraint(o, pltpu.VMEM) for o in outs))

    return jax.shard_map(
        per_device,
        mesh=mesh,
        in_specs=(
            P("section", "seq", None),
            P("section", None, "seq", None),
            P("section", None, None),
            P("section", None, None),
            P("section", "seq", None),
        ),
        out_specs=(
            P("section", "seq", None),
            P("section", "seq", None),
            P("section", None, "seq", None),
        ),
        check_vma=False,
    )
```
